32 devices in a mesh: prow: 4 (over y, core), pcol: 8 (over z, x).
Axes of the slice: x: 2, y: 2, z: 4, core: 2. Of those that a mesh axis runs over, the one named last changes fastest.
Arguments:
- matrix: bfloat16 [4096, 2048], P('prow', 'pcol'), may hold values from -6 to 6
- panel_one: bfloat16 [256, 4096], P('pcol', 'prow'), may hold values from -0.375 to 0.375
- panel_two: bfloat16 [256, 4096], P('pcol', 'prow'), may hold values from -0.375 to 0.375
- pivots_one: int32 [256], replicated, may hold values from 0 to 4095, as said below
- pivots_two: int32 [256], replicated, may hold values from 256 to 4095, as said below
Outputs:
- trailing: bfloat16 [4096, 2048], P('prow', 'pcol')
The draws below stay inside these ranges and needn't reach their ends.
Inputs may be any that keep to these rules, and one draw needn't show every extreme that they name: Each pivots_one[i] is either i or a logical row from 256 to 4095; no row is named twice; 4095 is always named. Each pivots_two[i] is either 256 + i or a logical row from 512 to 4095; no row is named twice; 4095 is always named.
All inputs are finite; a program needn't handle non-finite values.
Results may differ from the reference program's by a relative error of at most 0.006.
Values may be sent and summed in bfloat16 or wider, within the bound.
A program may use at most 64 MiB of HBM per device.

```python
import jax
import jax.numpy as jnp
from jax import lax

PANEL = 256
ROWS_DEV = 1024
PROWS = 4
ROWS = 4096
COLS = 2048


def choose_pivots(key, first_row):
    span_rows = ROWS - first_row - PANEL
    shuffled = jax.random.permutation(jax.random.fold_in(key, 31), span_rows - 1)[:PANEL]
    forced = jax.random.randint(jax.random.fold_in(key, 32), (), 0, PANEL)
    position = jnp.arange(PANEL, dtype=jnp.int32)
    shuffled = jnp.where(position == forced, span_rows - 1, shuffled)
    unmoved = (jax.random.randint(jax.random.fold_in(key, 33), (PANEL,), 0, 8) == 0) & (position != forced)
    return jnp.where(unmoved, first_row + position, first_row + PANEL + shuffled).astype(jnp.int32)


def panel_values(key):
    values = jnp.clip(jax.random.normal(key, (PANEL, ROWS), jnp.float32) * 0.0625, -0.375, 0.375)
    return values.astype(jnp.bfloat16)


def draw_panel_one(key, part):
    return panel_values(jax.random.fold_in(key, 11))


def draw_panel_two(key, part):
    return panel_values(jax.random.fold_in(key, 12))


def draw_pivots_one(key, part):
    return choose_pivots(jax.random.fold_in(key, 21), 0)


def draw_pivots_two(key, part):
    return choose_pivots(jax.random.fold_in(key, 22), PANEL)


def levels(own_key, dims, pieces, smallest, high):
    level, own = 1.0, jax.random.fold_in(own_key, 6)
    for axis_at, parts in pieces:
        steps = jnp.exp(jax.random.uniform(jax.random.fold_in(own, axis_at), (parts,), jnp.float32, smallest / len(pieces), high / len(pieces)))
        level = level * jnp.repeat(steps, dims[axis_at] // parts).reshape([-1 if axis == axis_at else 1 for axis in range(len(dims))])
    return level


def normal_values(own_key, shape, deviation, bound, cuts=(), kind=jnp.bfloat16):
    drawn = deviation * jax.random.normal(own_key, shape, jnp.float32)
    if cuts:
        drawn = drawn * levels(own_key, shape, cuts, -0.22, 0.18)
    return jnp.clip(drawn, -bound, bound).astype(kind)


def setup_inputs(seed: int = 0) -> dict:
    key_list = jax.random.split(jax.random.key(seed), 6)
    return {
        "matrix": normal_values(key_list[0], (ROWS, COLS), 1.0, 6.0, ((0, 4), (1, 8))),
        "panel_one": draw_panel_one(jax.random.fold_in(key_list[5], 71), 0),
        "panel_two": draw_panel_two(jax.random.fold_in(key_list[5], 71), 0),
        "pivots_one": draw_pivots_one(jax.random.fold_in(key_list[5], 71), 0),
        "pivots_two": draw_pivots_two(jax.random.fold_in(key_list[5], 71), 0),
    }


def stored_rows(logical):
    block_index = logical // PANEL
    return (block_index % PROWS) * ROWS_DEV + (block_index // PROWS) * PANEL + logical % PANEL


def unit_inverse(strict):
    extent = strict.shape[0]
    identity = jnp.eye(extent, dtype=jnp.float32)
    result = identity - strict
    powered = strict
    for repeat in range((extent - 1).bit_length() - 1):
        powered = jnp.dot(powered, powered, precision=lax.Precision.HIGHEST)
        result = jnp.dot(result, identity + powered, precision=lax.Precision.HIGHEST)
    return result


def reference(matrix, panel_one, panel_two, pivots_one, pivots_two):
    stored = jnp.arange(ROWS, dtype=jnp.int32)
    holder_row = stored // ROWS_DEV
    local_row = stored % ROWS_DEV
    logical = ((local_row // PANEL) * PROWS + holder_row) * PANEL + local_row % PANEL
    current = matrix
    sections = ((panel_one, pivots_one), (panel_two, pivots_two))
    for step_index in range(2):
        panel_now, pivots = sections[step_index]
        first_row = step_index * PANEL
        pivot_at = stored_rows(first_row + jnp.arange(PANEL, dtype=jnp.int32))
        chosen_at = stored_rows(pivots.astype(jnp.int32))
        leaving = current[pivot_at]
        arriving = current[chosen_at]
        current = current.at[chosen_at].set(leaving).at[pivot_at].set(arriving)
        pivot_rows = current[pivot_at].astype(jnp.float32)
        strict = jnp.tril(panel_now[:, pivot_at].T.astype(jnp.float32), -1)
        solved = jnp.dot(unit_inverse(strict), pivot_rows, precision=lax.Precision.HIGHEST).astype(jnp.bfloat16)

        def update_slab(operands, solved=solved, first_row=first_row):
            row_slab, panel_slab, logical_slab = operands
            product = jnp.dot(panel_slab.T.astype(jnp.float32), solved.astype(jnp.float32), precision=lax.Precision.HIGHEST)
            updated = (row_slab.astype(jnp.float32) - product).astype(jnp.bfloat16)
            pivot_part = jnp.take(solved, jnp.clip(logical_slab - first_row, 0, PANEL - 1), axis=0)
            beyond = logical_slab >= first_row + PANEL
            in_block = (logical_slab >= first_row) & (logical_slab < first_row + PANEL)
            return jnp.where(beyond[:, None], updated, jnp.where(in_block[:, None], pivot_part, row_slab))

        slabs = (current.reshape(PROWS, ROWS_DEV, COLS), panel_now.reshape(PANEL, PROWS, ROWS_DEV).transpose(1, 0, 2), logical.reshape(PROWS, ROWS_DEV))
        current = lax.map(update_slab, slabs).reshape(ROWS, COLS)
    return current
```

```python
import functools

import jax
import jax.numpy as jnp
from jax import lax
from jax.experimental import pallas as pl
from jax.experimental.pallas import tpu as pltpu
from jax.sharding import PartitionSpec as P

F32 = jnp.float32
BF16 = jnp.bfloat16
ROW_ROW = (((0,), (0,)), ((), ()))


def dot(a, b):
    return jnp.dot(a, b, preferred_element_type=F32)


def dot_t(a, b):
    return lax.dot_general(a, b, ROW_ROW, preferred_element_type=F32)


def halves(a):
    high = a.astype(BF16)
    return high, (a - high.astype(F32)).astype(BF16)


def dot_split(a, b):
    a_high, a_low = halves(a)
    b_high, b_low = halves(b)
    return dot(a_high, b_high) + (dot(a_high, b_low) + dot(a_low, b_high))


def unit_inverse(diagonal):
    extent = diagonal.shape[0]
    row = lax.broadcasted_iota(jnp.int32, (extent, extent), 0)
    col = lax.broadcasted_iota(jnp.int32, (extent, extent), 1)
    strict = jnp.where(row > col, diagonal.astype(F32).T, 0.0)
    exact = strict.astype(BF16)
    powered = dot(exact, exact)
    result = jnp.where(row == col, 1.0, 0.0) - strict
    repeats = (extent - 1).bit_length() - 1
    for repeat in range(repeats):
        if repeat == repeats - 1:
            return result + dot_split(result, powered)
        both = dot_split(jnp.concatenate([result, powered], axis=0), powered)
        result, powered = result + both[:extent], both[extent:]
    return result


def solve(inverse, incoming):
    high, low = halves(inverse)
    return (dot(high, incoming) + dot(low, incoming)).astype(BF16)


def onehot(a, b):
    return (a == b).astype(F32)


def body(
    process_rows, process_cols,
    matrix, panel_one, panel_two, piv_one, piv_two, out,
    gathered, sent_rows, rows_in, block_in, sent_sel, sel_in, aux,
    g_send, g_recv, f_send, r_send, r_recv, b_send, b_recv, s_send, s_recv, d_send, d_recv,
):
    width = piv_one.shape[1]
    rows_dev = matrix.shape[0]
    shard = panel_one.shape[0]
    size_z = process_cols // 2
    my_row = lax.axis_index("prow")
    my_col = lax.axis_index("pcol")
    my_z, my_x = my_col // 2, my_col % 2
    x_peer = my_z * 2 + (1 - my_x)

    def row_peer(step):
        return lax.rem(my_row + step, process_rows)

    def z_peer(step):
        return lax.rem(my_z + step, size_z) * 2 + my_x

    barrier = pltpu.get_barrier_semaphore()
    for step in range(1, process_rows):
        pl.semaphore_signal(barrier, 1, device_id={"prow": row_peer(step)}, device_id_type=pl.DeviceIdType.MESH)
    for step in range(1, size_z):
        pl.semaphore_signal(barrier, 1, device_id={"pcol": z_peer(step)}, device_id_type=pl.DeviceIdType.MESH)
    pl.semaphore_signal(barrier, 1, device_id={"pcol": x_peer}, device_id_type=pl.DeviceIdType.MESH)

    local = lax.broadcasted_iota(jnp.int32, (rows_dev, width), 0)
    logical = (local // width * process_rows + my_row) * width + local % width
    hit_one = onehot(logical, piv_one[...])
    hit_two = onehot(logical, piv_two[...])
    pick_one, pick_two = hit_one.astype(BF16), hit_two.astype(BF16)
    sent_sel[...] = dot(panel_one[...], pick_two).astype(BF16)
    gathered[0, my_col] = panel_one[...]
    gathered[2, my_col] = panel_two[...]

    pl.semaphore_wait(barrier, process_rows - 1 + size_z)

    def remote(src, dst, send, recv, device):
        return pltpu.make_async_remote_copy(
            src_ref=src, dst_ref=dst, send_sem=send, recv_sem=recv,
            device_id=device, device_id_type=pl.DeviceIdType.MESH,
        )

    def sel_copy(step):
        return remote(sent_sel, sel_in.at[my_row], s_send.at[step], s_recv.at[my_row], {"prow": row_peer(step)})

    def fixed_copy(which, step):
        src = (panel_one, panel_one, panel_two)[which].at[:, pl.ds(0, width)]
        dst = aux.at[which]
        return remote(src, dst, d_send.at[which, step], d_recv.at[which], {"prow": row_peer(step)})

    def block_copy(which, step):
        src = matrix.at[pl.ds(0, width), :]
        return remote(src, block_in.at[which], b_send.at[which, step], b_recv.at[which], {"prow": row_peer(step)})

    def rows_copy(which, step):
        return remote(
            sent_rows.at[which], rows_in.at[which, my_row],
            r_send.at[which, step], r_recv.at[which, my_row], {"prow": row_peer(step)},
        )

    def gather_copy(array, step):
        dst = gathered.at[array, my_col]
        device = {"pcol": z_peer(step) if step else x_peer}
        return remote(dst, dst, g_send.at[array, step], g_recv.at[array, my_col], device)

    def forward_copy(array, step):
        slot = gathered.at[array, z_peer(step)]
        return remote(slot, slot, f_send.at[array, step], g_recv.at[array, z_peer(step)], {"pcol": x_peer})

    def arrive(array, col):
        slot = gathered.at[array, col]
        remote(slot, slot, g_send.at[array, 0], g_recv.at[array, col], {"pcol": x_peer}).wait_recv()

    peers = range(1, process_rows)
    holders = (0, 1, 1)
    for step in peers:
        sel_copy(step).start()
    for which in range(3):
        @pl.when(my_row == holders[which])
        def _(which=which):
            for step in peers:
                fixed_copy(which, step).start()
            aux[which] = (panel_one, panel_one, panel_two)[which][:, pl.ds(0, width)]

    for step in range(size_z):
        gather_copy(0, step).start()

    sent_rows[0] = dot_t(pick_one, matrix[...]).astype(BF16)
    for step in peers:
        rows_copy(0, step).start()
    sent_rows[1] = dot_t(pick_two, matrix[...]).astype(BF16)
    for step in peers:
        rows_copy(1, step).start()
    for which in range(2):
        @pl.when(my_row == which)
        def _(which=which):
            for step in peers:
                block_copy(which, step).start()
            block_in[which] = matrix[pl.ds(0, width), :]

    selected = sent_sel[...].astype(F32)
    for step in peers:
        source = row_peer(step)
        slot = sel_in.at[source]
        remote(slot, slot, s_send.at[0], s_recv.at[source], {"prow": source}).wait_recv()
        selected = selected + sel_in[source].astype(F32)
    for which in range(3):
        @pl.when(my_row != holders[which])
        def _(which=which):
            slot = aux.at[which]
            remote(slot, slot, d_send.at[which, 0], d_recv.at[which], {"prow": row_peer(1)}).wait_recv()
    for which in range(3):
        gathered[1, my_col, :, pl.ds(which * width, width)] = aux[which]
    gathered[1, my_col, :, pl.ds(3 * width, width)] = selected.astype(BF16)
    for array in (1, 2):
        for step in range(size_z):
            gather_copy(array, step).start()

    def take_z(array):
        for step in range(1, size_z):
            arrive(array, z_peer(step))
            forward_copy(array, step).start()

    def take_x(array):
        for step in range(size_z):
            arrive(array, lax.rem(my_z + step, size_z) * 2 + (1 - my_x))

    def whole(array, start, count):
        return gathered[array, :, :, pl.ds(start, count)].reshape(process_cols * shard, count)

    take_z(0)
    take_z(1)
    take_x(1)
    inverse_one = unit_inverse(whole(1, 0, width))
    inverse_two = unit_inverse(whole(1, 2 * width, width))
    take_z(2)

    def summed(which):
        total = sent_rows[which].astype(F32)
        for step in peers:
            source = row_peer(step)
            slot = rows_in.at[which, source]
            remote(slot, slot, r_send.at[which, 0], r_recv.at[which, source], {"prow": source}).wait_recv()
            total = total + rows_in[which, source].astype(F32)
        return total

    for which in range(2):
        @pl.when(my_row != which)
        def _(which=which):
            slot = block_in.at[which]
            remote(slot, slot, b_send.at[which, 0], b_recv.at[which], {"prow": row_peer(1)}).wait_recv()

    solved_one = solve(inverse_one, summed(0).astype(BF16))
    leaving_one = block_in[0]

    first_row = width
    first_across = jnp.broadcast_to(piv_one[...], (width, width))
    second_down = jnp.broadcast_to(piv_two[...].astype(F32), (width, width)).T.astype(jnp.int32)
    block_down = first_row + lax.broadcasted_iota(jnp.int32, (width, width), 0)

    def after_one(base, names, columns):
        match = onehot(names, first_across)
        moved = jnp.sum(match, axis=1, keepdims=True)
        swapped = base * (1.0 - moved) + dot(match.astype(BF16), leaving_one)
        return (swapped - dot_t(columns, solved_one)).astype(BF16)

    incoming_two = after_one(summed(1), second_down, whole(1, 3 * width, width))
    leaving_two = after_one(block_in[1].astype(F32), block_down, whole(1, width, width))
    solved_two = solve(inverse_two, incoming_two)

    take_x(0)
    moved_one = jnp.sum(hit_one, axis=1, keepdims=True)
    moved_two = jnp.sum(hit_two, axis=1, keepdims=True)
    swapped = matrix[...].astype(F32) * (1.0 - moved_one) + dot(pick_one, leaving_one)
    current = (swapped - dot_t(whole(0, 0, rows_dev), solved_one)).astype(BF16).astype(F32)
    swapped = current * (1.0 - moved_two) + dot(pick_two, leaving_two)
    take_x(2)
    out[...] = (swapped - dot_t(whole(2, 0, rows_dev), solved_two)).astype(BF16)

    @pl.when(my_row == 0)
    def _():
        out[pl.ds(0, width), :] = solved_one

    @pl.when(my_row == 1)
    def _():
        out[pl.ds(0, width), :] = solved_two

    for step in peers:
        sel_copy(step).wait_send()
        rows_copy(0, step).wait_send()
        rows_copy(1, step).wait_send()
    for which in range(3):
        @pl.when(my_row == holders[which])
        def _(which=which):
            for step in peers:
                fixed_copy(which, step).wait_send()
    for which in range(2):
        @pl.when(my_row == which)
        def _(which=which):
            for step in peers:
                block_copy(which, step).wait_send()
    for array in range(3):
        for step in range(size_z):
            gather_copy(array, step).wait_send()
        for step in range(1, size_z):
            forward_copy(array, step).wait_send()


def on_device(matrix, panel_one, panel_two, pivots_one, pivots_two):
    process_rows = lax.axis_size("prow")
    process_cols = lax.axis_size("pcol")
    shard, rows_dev = panel_one.shape
    width = pivots_one.shape[0]
    cols = matrix.shape[1]
    vmem = pl.BlockSpec(memory_space=pltpu.VMEM)
    dma = pltpu.SemaphoreType.DMA
    assert 4 * width == rows_dev and shard * process_cols == width and process_cols % 2 == 0
    size_z = process_cols // 2
    return pl.pallas_call(
        functools.partial(body, process_rows, process_cols),
        out_shape=jax.ShapeDtypeStruct(matrix.shape, BF16),
        in_specs=[vmem] * 5,
        out_specs=vmem,
        scratch_shapes=[
            pltpu.VMEM((3, process_cols, shard, rows_dev), BF16),
            pltpu.VMEM((2, width, cols), BF16),
            pltpu.VMEM((2, process_rows, width, cols), BF16),
            pltpu.VMEM((2, width, cols), BF16),
            pltpu.VMEM((shard, width), BF16),
            pltpu.VMEM((process_rows, shard, width), BF16),
            pltpu.VMEM((3, shard, width), BF16),
            dma((3, size_z)), dma((3, process_cols)), dma((3, size_z)),
            dma((2, process_rows)), dma((2, process_rows)),
            dma((2, process_rows)), dma((2,)),
            dma((process_rows,)), dma((process_rows,)),
            dma((3, process_rows)), dma((3,)),
        ],
        compiler_params=pltpu.CompilerParams(
            collective_id=0, has_side_effects=True, vmem_limit_bytes=40 * 1024 * 1024
        ),
    )(matrix, panel_one, panel_two, pivots_one.reshape(1, width), pivots_two.reshape(1, width))


def solution(mesh):
    placed = (P("prow", "pcol"), P("pcol", "prow"), P("pcol", "prow"), P(), P())
    return jax.shard_map(
        on_device, mesh=mesh, in_specs=placed, out_specs=P("prow", "pcol"), check_vma=False
    )
```

```python
import functools

import jax
import jax.numpy as jnp
from jax import lax
from jax.experimental import pallas as pl
from jax.experimental.pallas import tpu as pltpu
from jax.sharding import PartitionSpec as P

F32 = jnp.float32
BF16 = jnp.bfloat16
ROW_ROW = (((0,), (0,)), ((), ()))


def dot(a, b):
    return jnp.dot(a, b, preferred_element_type=F32)


def dot_t(a, b):
    return lax.dot_general(a, b, ROW_ROW, preferred_element_type=F32)


def halves(a):
    high = a.astype(BF16)
    return high, (a - high.astype(F32)).astype(BF16)


def dot_split(a, b):
    a_high, a_low = halves(a)
    b_high, b_low = halves(b)
    return dot(a_high, b_high) + (dot(a_high, b_low) + dot(a_low, b_high))


def unit_inverse(diagonal):
    extent = diagonal.shape[0]
    row = lax.broadcasted_iota(jnp.int32, (extent, extent), 0)
    col = lax.broadcasted_iota(jnp.int32, (extent, extent), 1)
    strict = jnp.where(row > col, diagonal.astype(F32).T, 0.0)
    exact = strict.astype(BF16)
    powered = dot(exact, exact)
    result = jnp.where(row == col, 1.0, 0.0) - strict
    repeats = (extent - 1).bit_length() - 1
    for repeat in range(repeats):
        if repeat == repeats - 1:
            return result + dot_split(result, powered)
        both = dot_split(jnp.concatenate([result, powered], axis=0), powered)
        result, powered = result + both[:extent], both[extent:]
    return result


def solve(inverse, incoming):
    high, low = halves(inverse)
    return (dot(high, incoming) + dot(low, incoming)).astype(BF16)


def onehot(a, b):
    return (a == b).astype(F32)


def body(
    process_rows, process_cols,
    matrix_hbm, one_hbm, two_hbm, piv_one, piv_two, out,
    matrix, head, tail, sent_sel, sel_in, item_in,
    sent_rows, pair_rows, group_rows, full_rows,
    l_sem, gh_send, gh_recv, fh_send, gt_send, gt_recv, ft_send, s_send, s_recv, i_send, i_recv,
    p_send, p_recv, q_send, q_recv, h_send, h_recv,
):
    width = piv_one.shape[1]
    rows_dev = matrix.shape[0]
    shard = one_hbm.shape[0]
    half = width // 2
    size_z = process_cols // 2
    groups = process_rows // 2
    my_row = lax.axis_index("prow")
    my_col = lax.axis_index("pcol")
    my_z, my_x = my_col // 2, my_col % 2
    x_peer = my_z * 2 + (1 - my_x)
    group, core = my_row // 2, my_row % 2
    pair = group * 2 + (1 - core)
    mesh_ids = pl.DeviceIdType.MESH

    def row_peer(step):
        return lax.rem(my_row + step, process_rows)

    def group_peer(step):
        return lax.rem(group + step, groups) * 2 + core

    def z_peer(step):
        return lax.rem(my_z + step, size_z) * 2 + my_x

    barrier = pltpu.get_barrier_semaphore()
    for step in range(1, process_rows):
        pl.semaphore_signal(barrier, 1, device_id={"prow": row_peer(step)}, device_id_type=mesh_ids)
    for step in range(1, size_z):
        pl.semaphore_signal(barrier, 1, device_id={"pcol": z_peer(step)}, device_id_type=mesh_ids)
    pl.semaphore_signal(barrier, 1, device_id={"pcol": x_peer}, device_id_type=mesh_ids)

    first, rest = pl.ds(0, width), pl.ds(width, rows_dev - width)
    loads = [
        pltpu.make_async_copy(one_hbm.at[:, first], head.at[0, my_col], l_sem.at[0]),
        pltpu.make_async_copy(one_hbm.at[:, rest], tail.at[0, my_col], l_sem.at[1]),
        pltpu.make_async_copy(two_hbm.at[:, first], head.at[1, my_col], l_sem.at[2]),
        pltpu.make_async_copy(matrix_hbm, matrix, l_sem.at[3]),
        pltpu.make_async_copy(two_hbm.at[:, rest], tail.at[1, my_col], l_sem.at[4]),
    ]
    for load in loads:
        load.start()

    local = lax.broadcasted_iota(jnp.int32, (rows_dev, width), 0)
    logical = (local // width * process_rows + my_row) * width + local % width
    hit_one = onehot(logical, piv_one[...])
    hit_two = onehot(logical, piv_two[...])
    pick_one, pick_two = hit_one.astype(BF16), hit_two.astype(BF16)
    for load in loads:
        load.wait()
    sent_sel[...] = (dot(head[0, my_col], pick_two[:width]) + dot(tail[0, my_col], pick_two[width:])).astype(BF16)

    pl.semaphore_wait(barrier, process_rows - 1 + size_z)

    def remote(src, dst, send, recv, device):
        return pltpu.make_async_remote_copy(
            src_ref=src, dst_ref=dst, send_sem=send, recv_sem=recv,
            device_id=device, device_id_type=mesh_ids,
        )

    def slot_of(piece, col):
        if piece < 3:
            return head.at[piece, col], gh_send.at[piece], gh_recv.at[piece, col], fh_send.at[piece]
        return tail.at[piece - 3, col], gt_send.at[piece - 3], gt_recv.at[piece - 3, col], ft_send.at[piece - 3]

    def gather_copy(piece, step):
        slot, send, recv, _ = slot_of(piece, my_col)
        return remote(slot, slot, send.at[step], recv, {"pcol": z_peer(step) if step else x_peer})

    def forward_copy(piece, step):
        slot, _, recv, send = slot_of(piece, z_peer(step))
        return remote(slot, slot, send.at[step], recv, {"pcol": x_peer})

    def gather(piece):
        for step in range(size_z):
            gather_copy(piece, step).start()

    def arrive(piece, col):
        slot, send, recv, _ = slot_of(piece, col)
        remote(slot, slot, send.at[0], recv, {"pcol": x_peer}).wait_recv()

    def take_z(piece):
        for step in range(1, size_z):
            arrive(piece, z_peer(step))
            forward_copy(piece, step).start()

    def take_x(piece):
        for step in range(size_z):
            arrive(piece, lax.rem(my_z + step, size_z) * 2 + (1 - my_x))

    def flat(block):
        return block.reshape(process_cols * shard, block.shape[-1])

    def sel_copy(step):
        return remote(sent_sel, sel_in.at[my_row], s_send.at[step], s_recv.at[my_row], {"prow": row_peer(step)})

    owners = (0, 1, 1, 0, 1)

    def item_source(item):
        if item < 3:
            return head.at[(0, 1, 0)[item]]
        return matrix.at[first, :]

    def item_place(item):
        return item_in[0].at[item] if item < 3 else item_in[1].at[item - 3]

    def item_copy(item, step, source):
        device = {"prow": group_peer(step) if step else pair}
        return remote(source, item_place(item), i_send.at[item, step], i_recv.at[item], device)

    def send_item(item):
        @pl.when(my_row == owners[item])
        def _():
            for step in range(groups):
                item_copy(item, step, item_source(item)).start()
            if item < 3:
                item_in[0][item] = head[(0, 1, 0)[item]]
            else:
                item_in[1][item - 3] = matrix[first, :]

    def take_item(item):
        @pl.when(my_row != owners[item])
        def _():
            item_copy(item, 0, item_place(item)).wait_recv()

        @pl.when((group > 0) & (core == owners[item]))
        def _():
            item_copy(item, 0, item_place(item)).start()

    def pair_copy(which):
        return remote(sent_rows.at[which, 1 - core], pair_rows.at[which], p_send.at[which], p_recv.at[which], {"prow": pair})

    def group_copy(which, step):
        return remote(
            sent_rows.at[which, core], group_rows.at[which, group],
            q_send.at[which, step], q_recv.at[which, group], {"prow": group_peer(step)},
        )

    def half_copy(which):
        return remote(
            full_rows.at[which, core], full_rows.at[which, core], h_send.at[which], h_recv.at[which], {"prow": pair}
        )

    def sum_pair(which):
        slot = pair_rows.at[which]
        remote(slot, slot, p_send.at[which], p_recv.at[which], {"prow": pair}).wait_recv()
        total = sent_rows[which, core].astype(F32) + pair_rows[which].astype(F32)
        sent_rows[which, core] = total.astype(BF16)
        for step in range(1, groups):
            group_copy(which, step).start()

    def sum_groups(which):
        total = sent_rows[which, core].astype(F32)
        for step in range(1, groups):
            source = lax.rem(group + step, groups)
            slot = group_rows.at[which, source]
            remote(slot, slot, q_send.at[which, 0], q_recv.at[which, source], {"prow": pair}).wait_recv()
            total = total + group_rows[which, source].astype(F32)
        full_rows[which, core] = total.astype(BF16)
        half_copy(which).start()

    def chosen(which):
        slot = full_rows.at[which, 1 - core]
        remote(slot, slot, h_send.at[which], h_recv.at[which], {"prow": pair}).wait_recv()
        return full_rows[which].reshape(width, full_rows.shape[-1])

    peers = range(1, process_rows)
    gather(0)
    gather(1)
    for step in peers:
        sel_copy(step).start()
    for which, pick in enumerate((pick_one, pick_two)):
        sent_rows[which] = dot_t(pick, matrix[...]).astype(BF16).reshape(2, half, matrix.shape[1])
        pair_copy(which).start()
    gather(3)
    take_z(0)
    take_z(1)
    sum_pair(0)
    sum_pair(1)
    selected = sent_sel[...].astype(F32)
    for step in peers:
        source = row_peer(step)
        slot = sel_in.at[source]
        remote(slot, slot, s_send.at[0], s_recv.at[source], {"prow": source}).wait_recv()
        selected = selected + sel_in[source].astype(F32)
    head[2, my_col] = selected.astype(BF16)
    gather(2)
    gather(4)
    take_x(0)
    send_item(0)
    take_x(1)
    send_item(1)
    sum_groups(0)
    sum_groups(1)
    send_item(3)
    send_item(2)
    send_item(4)
    take_z(3)
    take_z(2)
    take_item(0)
    take_item(1)
    inverse_one = unit_inverse(flat(item_in[0][0]))
    take_z(4)
    inverse_two = unit_inverse(flat(item_in[0][1]))
    take_item(3)
    take_item(2)
    take_item(4)

    solved_one = solve(inverse_one, chosen(0))
    leaving_one = item_in[1][0]

    first_across = jnp.broadcast_to(piv_one[...], (width, width))
    second_down = jnp.broadcast_to(piv_two[...].astype(F32), (width, width)).T.astype(jnp.int32)
    block_down = width + lax.broadcasted_iota(jnp.int32, (width, width), 0)

    def after_one(base, names, columns):
        match = onehot(names, first_across)
        moved = jnp.sum(match, axis=1, keepdims=True)
        swapped = base.astype(F32) * (1.0 - moved) + dot(match.astype(BF16), leaving_one)
        return (swapped - dot_t(columns, solved_one)).astype(BF16)

    take_x(2)
    incoming_two = after_one(chosen(1), second_down, flat(head[2]))
    leaving_two = after_one(item_in[1][1], block_down, flat(item_in[0][2]))
    solved_two = solve(inverse_two, incoming_two)

    moved_one = jnp.sum(hit_one, axis=1, keepdims=True)
    moved_two = jnp.sum(hit_two, axis=1, keepdims=True)
    swapped = matrix[...].astype(F32) * (1.0 - moved_one) + dot(pick_one, leaving_one)

    def times(which, solved):
        return jnp.concatenate([dot_t(flat(head[which]), solved), dot_t(flat(tail[which]), solved)], axis=0)

    take_x(3)
    current = (swapped - times(0, solved_one)).astype(BF16).astype(F32)
    swapped = current * (1.0 - moved_two) + dot(pick_two, leaving_two)
    take_x(4)
    out[...] = (swapped - times(1, solved_two)).astype(BF16)

    @pl.when(my_row == 0)
    def _():
        out[first, :] = solved_one

    @pl.when(my_row == 1)
    def _():
        out[first, :] = solved_two

    for step in peers:
        sel_copy(step).wait_send()
    for piece in range(5):
        for step in range(size_z):
            gather_copy(piece, step).wait_send()
        for step in range(1, size_z):
            forward_copy(piece, step).wait_send()
    for which in range(2):
        pair_copy(which).wait_send()
        half_copy(which).wait_send()
        for step in range(1, groups):
            group_copy(which, step).wait_send()
    for item in range(5):
        @pl.when(my_row == owners[item])
        def _(item=item):
            for step in range(groups):
                item_copy(item, step, item_source(item)).wait_send()

        @pl.when((group > 0) & (core == owners[item]))
        def _(item=item):
            item_copy(item, 0, item_place(item)).wait_send()


def on_device(matrix, panel_one, panel_two, pivots_one, pivots_two):
    process_rows = lax.axis_size("prow")
    process_cols = lax.axis_size("pcol")
    shard, rows_dev = panel_one.shape
    width = pivots_one.shape[0]
    cols = matrix.shape[1]
    vmem = pl.BlockSpec(memory_space=pltpu.VMEM)
    hbm = pl.BlockSpec(memory_space=pltpu.HBM)
    dma = pltpu.SemaphoreType.DMA
    assert rows_dev > width and shard * process_cols == width
    assert process_cols % 2 == 0 and process_rows % 2 == 0
    size_z = process_cols // 2
    groups = process_rows // 2
    half = width // 2
    return pl.pallas_call(
        functools.partial(body, process_rows, process_cols),
        out_shape=jax.ShapeDtypeStruct(matrix.shape, BF16),
        in_specs=[hbm] * 3 + [vmem] * 2,
        out_specs=vmem,
        scratch_shapes=[
            pltpu.VMEM((rows_dev, cols), BF16),
            pltpu.VMEM((3, process_cols, shard, width), BF16),
            pltpu.VMEM((2, process_cols, shard, rows_dev - width), BF16),
            pltpu.VMEM((shard, width), BF16),
            pltpu.VMEM((process_rows, shard, width), BF16),
            [pltpu.VMEM((3, process_cols, shard, width), BF16), pltpu.VMEM((2, width, cols), BF16)],
            pltpu.VMEM((2, 2, half, cols), BF16),
            pltpu.VMEM((2, half, cols), BF16),
            pltpu.VMEM((2, groups, half, cols), BF16),
            pltpu.VMEM((2, 2, half, cols), BF16),
            dma((5,)),
            dma((3, size_z)), dma((3, process_cols)), dma((3, size_z)),
            dma((2, size_z)), dma((2, process_cols)), dma((2, size_z)),
            dma((process_rows,)), dma((process_rows,)),
            dma((5, groups)), dma((5,)),
            dma((2,)), dma((2,)),
            dma((2, groups)), dma((2, groups)),
            dma((2,)), dma((2,)),
        ],
        compiler_params=pltpu.CompilerParams(
            collective_id=0, has_side_effects=True, vmem_limit_bytes=40 * 1024 * 1024
        ),
    )(matrix, panel_one, panel_two, pivots_one.reshape(1, width), pivots_two.reshape(1, width))


def solution(mesh):
    placed = (P("prow", "pcol"), P("pcol", "prow"), P("pcol", "prow"), P(), P())
    return jax.shard_map(
        on_device, mesh=mesh, in_specs=placed, out_specs=P("prow", "pcol"), check_vma=False
    )
```

```python
import functools

import jax
import jax.numpy as jnp
from jax import lax
from jax.experimental import pallas as pl
from jax.experimental.pallas import tpu as pltpu
from jax.sharding import PartitionSpec as P

F32 = jnp.float32
BF16 = jnp.bfloat16
ROW_ROW = (((0,), (0,)), ((), ()))


def dot(a, b):
    return jnp.dot(a, b, preferred_element_type=F32)


def dot_t(a, b):
    return lax.dot_general(a, b, ROW_ROW, preferred_element_type=F32)


def halves(a):
    high = a.astype(BF16)
    return high, (a - high.astype(F32)).astype(BF16)


def dot_split(a, b):
    a_high, a_low = halves(a)
    b_high, b_low = halves(b)
    return dot(a_high, b_high) + (dot(a_high, b_low) + dot(a_low, b_high))


def unit_inverses(diagonals):
    extent = diagonals[0].shape[0]
    row = lax.broadcasted_iota(jnp.int32, (extent, extent), 0)
    col = lax.broadcasted_iota(jnp.int32, (extent, extent), 1)
    stricts = [jnp.where(row > col, d.astype(F32).T, 0.0) for d in diagonals]
    powers = [dot(s.astype(BF16), s.astype(BF16)) for s in stricts]
    results = [jnp.where(row == col, 1.0, 0.0) - s for s in stricts]
    repeats = (extent - 1).bit_length() - 1
    for repeat in range(repeats):
        if repeat == repeats - 1:
            return [r + dot_split(r, p) for r, p in zip(results, powers)]
        both = [dot_split(jnp.concatenate([r, p], axis=0), p) for r, p in zip(results, powers)]
        results = [r + b[:extent] for r, b in zip(results, both)]
        powers = [b[extent:] for b in both]


def unit_inverse(diagonal):
    extent = diagonal.shape[0]
    row = lax.broadcasted_iota(jnp.int32, (extent, extent), 0)
    col = lax.broadcasted_iota(jnp.int32, (extent, extent), 1)
    strict = jnp.where(row > col, diagonal.astype(F32).T, 0.0)
    exact = strict.astype(BF16)
    powered = dot(exact, exact)
    result = jnp.where(row == col, 1.0, 0.0) - strict
    repeats = (extent - 1).bit_length() - 1
    for repeat in range(repeats):
        if repeat == repeats - 1:
            return result + dot_split(result, powered)
        both = dot_split(jnp.concatenate([result, powered], axis=0), powered)
        result, powered = result + both[:extent], both[extent:]
    return result


def solve(inverse, incoming):
    high, low = halves(inverse)
    return (dot(high, incoming) + dot(low, incoming)).astype(BF16)


def onehot(a, b):
    return (a == b).astype(F32)


def body(
    process_rows, process_cols,
    matrix_hbm, one_hbm, two_hbm, piv_one, piv_two, out,
    matrix, head, tail, sent_sel, sel_in, item_in,
    sent_rows, pair_rows, group_rows, full_rows,
    l_sem, gh_send, gh_recv, fh_send, gt_send, gt_recv, ft_send, s_send, s_recv, i_send, i_recv,
    p_send, p_recv, q_send, q_recv, h_send, h_recv,
):
    width = piv_one.shape[1]
    rows_dev = matrix.shape[0]
    shard = one_hbm.shape[0]
    half = width // 2
    size_z = process_cols // 2
    groups = process_rows // 2
    my_row = lax.axis_index("prow")
    my_col = lax.axis_index("pcol")
    my_z, my_x = my_col // 2, my_col % 2
    x_peer = my_z * 2 + (1 - my_x)
    group, core = my_row // 2, my_row % 2
    pair = group * 2 + (1 - core)
    mesh_ids = pl.DeviceIdType.MESH

    def row_peer(step):
        return lax.rem(my_row + step, process_rows)

    def group_peer(step):
        return lax.rem(group + step, groups) * 2 + core

    def z_peer(step):
        return lax.rem(my_z + step, size_z) * 2 + my_x

    barrier = pltpu.get_barrier_semaphore()
    for step in range(1, process_rows):
        pl.semaphore_signal(barrier, 1, device_id={"prow": row_peer(step)}, device_id_type=mesh_ids)
    for step in range(1, size_z):
        pl.semaphore_signal(barrier, 1, device_id={"pcol": z_peer(step)}, device_id_type=mesh_ids)
    pl.semaphore_signal(barrier, 1, device_id={"pcol": x_peer}, device_id_type=mesh_ids)

    first, rest = pl.ds(0, width), pl.ds(width, rows_dev - width)
    loads = [
        pltpu.make_async_copy(one_hbm.at[:, first], head.at[0, my_col], l_sem.at[0]),
        pltpu.make_async_copy(one_hbm.at[:, rest], tail.at[0, my_col], l_sem.at[1]),
        pltpu.make_async_copy(two_hbm.at[:, first], head.at[1, my_col], l_sem.at[2]),
        pltpu.make_async_copy(matrix_hbm, matrix, l_sem.at[3]),
        pltpu.make_async_copy(two_hbm.at[:, rest], tail.at[1, my_col], l_sem.at[4]),
    ]
    for load in loads:
        load.start()

    local = lax.broadcasted_iota(jnp.int32, (rows_dev, width), 0)
    logical = (local // width * process_rows + my_row) * width + local % width
    hit_one = onehot(logical, piv_one[...])
    hit_two = onehot(logical, piv_two[...])
    pick_one, pick_two = hit_one.astype(BF16), hit_two.astype(BF16)
    for load in loads:
        load.wait()
    sent_sel[...] = (dot(head[0, my_col], pick_two[:width]) + dot(tail[0, my_col], pick_two[width:])).astype(BF16)

    pl.semaphore_wait(barrier, process_rows - 1 + size_z)

    def remote(src, dst, send, recv, device):
        return pltpu.make_async_remote_copy(
            src_ref=src, dst_ref=dst, send_sem=send, recv_sem=recv,
            device_id=device, device_id_type=mesh_ids,
        )

    def slot_of(piece, col):
        if piece < 3:
            return head.at[piece, col], gh_send.at[piece], gh_recv.at[piece, col], fh_send.at[piece]
        return tail.at[piece - 3, col], gt_send.at[piece - 3], gt_recv.at[piece - 3, col], ft_send.at[piece - 3]

    def gather_copy(piece, step):
        slot, send, recv, _ = slot_of(piece, my_col)
        return remote(slot, slot, send.at[step], recv, {"pcol": z_peer(step) if step else x_peer})

    def forward_copy(piece, step):
        slot, _, recv, send = slot_of(piece, z_peer(step))
        return remote(slot, slot, send.at[step], recv, {"pcol": x_peer})

    def gather(piece):
        for step in range(size_z):
            gather_copy(piece, step).start()

    def arrive(piece, col):
        slot, send, recv, _ = slot_of(piece, col)
        remote(slot, slot, send.at[0], recv, {"pcol": x_peer}).wait_recv()

    def take_z(piece):
        for step in range(1, size_z):
            arrive(piece, z_peer(step))
            forward_copy(piece, step).start()

    def take_x(piece):
        for step in range(size_z):
            arrive(piece, lax.rem(my_z + step, size_z) * 2 + (1 - my_x))

    def flat(block):
        return block.reshape(process_cols * shard, block.shape[-1])

    def sel_copy(step):
        return remote(sent_sel, sel_in.at[my_row], s_send.at[step], s_recv.at[my_row], {"prow": row_peer(step)})

    owners = (0, 1, 1, 0, 1)

    def item_source(item):
        if item < 3:
            return head.at[(0, 1, 0)[item]]
        return matrix.at[first, :]

    def item_place(item):
        return item_in[0].at[item] if item < 3 else item_in[1].at[item - 3]

    def item_copy(item, step, source):
        device = {"prow": group_peer(step) if step else pair}
        return remote(source, item_place(item), i_send.at[item, step], i_recv.at[item], device)

    def send_item(item):
        @pl.when(my_row == owners[item])
        def _():
            for step in range(groups):
                item_copy(item, step, item_source(item)).start()
            if item < 3:
                item_in[0][item] = head[(0, 1, 0)[item]]
            else:
                item_in[1][item - 3] = matrix[first, :]

    def take_item(item):
        @pl.when(my_row != owners[item])
        def _():
            item_copy(item, 0, item_place(item)).wait_recv()

        @pl.when((group > 0) & (core == owners[item]))
        def _():
            item_copy(item, 0, item_place(item)).start()

    def pair_copy(which):
        return remote(sent_rows.at[which, 1 - core], pair_rows.at[which], p_send.at[which], p_recv.at[which], {"prow": pair})

    def group_copy(which, step):
        return remote(
            sent_rows.at[which, core], group_rows.at[which, group],
            q_send.at[which, step], q_recv.at[which, group], {"prow": group_peer(step)},
        )

    def half_copy(which):
        return remote(
            full_rows.at[which, core], full_rows.at[which, core], h_send.at[which], h_recv.at[which], {"prow": pair}
        )

    def sum_pair(which):
        slot = pair_rows.at[which]
        remote(slot, slot, p_send.at[which], p_recv.at[which], {"prow": pair}).wait_recv()
        total = sent_rows[which, core].astype(F32) + pair_rows[which].astype(F32)
        sent_rows[which, core] = total.astype(BF16)
        for step in range(1, groups):
            group_copy(which, step).start()

    def sum_groups(which):
        total = sent_rows[which, core].astype(F32)
        for step in range(1, groups):
            source = lax.rem(group + step, groups)
            slot = group_rows.at[which, source]
            remote(slot, slot, q_send.at[which, 0], q_recv.at[which, source], {"prow": pair}).wait_recv()
            total = total + group_rows[which, source].astype(F32)
        full_rows[which, core] = total.astype(BF16)
        half_copy(which).start()

    def chosen(which):
        slot = full_rows.at[which, 1 - core]
        remote(slot, slot, h_send.at[which], h_recv.at[which], {"prow": pair}).wait_recv()
        return full_rows[which].reshape(width, full_rows.shape[-1])

    peers = range(1, process_rows)
    gather(0)
    gather(1)
    for step in peers:
        sel_copy(step).start()
    for which, pick in enumerate((pick_one, pick_two)):
        sent_rows[which] = dot_t(pick, matrix[...]).astype(BF16).reshape(2, half, matrix.shape[1])
        pair_copy(which).start()
    gather(3)
    take_z(0)
    take_z(1)
    sum_pair(0)
    sum_pair(1)
    selected = sent_sel[...].astype(F32)
    for step in peers:
        source = row_peer(step)
        slot = sel_in.at[source]
        remote(slot, slot, s_send.at[0], s_recv.at[source], {"prow": source}).wait_recv()
        selected = selected + sel_in[source].astype(F32)
    head[2, my_col] = selected.astype(BF16)
    gather(2)
    gather(4)
    take_x(0)
    send_item(0)
    take_x(1)
    send_item(1)
    sum_groups(0)
    sum_groups(1)
    send_item(3)
    send_item(2)
    send_item(4)
    take_z(3)
    take_z(2)
    take_item(0)
    take_item(1)
    take_z(4)
    inverse_one, inverse_two = unit_inverses([flat(item_in[0][0]), flat(item_in[0][1])])
    take_item(3)
    take_item(2)
    take_item(4)

    solved_one = solve(inverse_one, chosen(0))
    leaving_one = item_in[1][0]

    first_across = jnp.broadcast_to(piv_one[...], (width, width))
    second_down = jnp.broadcast_to(piv_two[...].astype(F32), (width, width)).T.astype(jnp.int32)
    block_down = width + lax.broadcasted_iota(jnp.int32, (width, width), 0)

    def after_one(base, names, columns):
        match = onehot(names, first_across)
        moved = jnp.sum(match, axis=1, keepdims=True)
        swapped = base.astype(F32) * (1.0 - moved) + dot(match.astype(BF16), leaving_one)
        return (swapped - dot_t(columns, solved_one)).astype(BF16)

    take_x(2)
    incoming_two = after_one(chosen(1), second_down, flat(head[2]))
    leaving_two = after_one(item_in[1][1], block_down, flat(item_in[0][2]))
    solved_two = solve(inverse_two, incoming_two)

    moved_one = jnp.sum(hit_one, axis=1, keepdims=True)
    moved_two = jnp.sum(hit_two, axis=1, keepdims=True)
    swapped = matrix[...].astype(F32) * (1.0 - moved_one) + dot(pick_one, leaving_one)

    def times(which, solved):
        return jnp.concatenate([dot_t(flat(head[which]), solved), dot_t(flat(tail[which]), solved)], axis=0)

    take_x(3)
    current = (swapped - times(0, solved_one)).astype(BF16).astype(F32)
    swapped = current * (1.0 - moved_two) + dot(pick_two, leaving_two)
    take_x(4)
    out[...] = (swapped - times(1, solved_two)).astype(BF16)

    @pl.when(my_row == 0)
    def _():
        out[first, :] = solved_one

    @pl.when(my_row == 1)
    def _():
        out[first, :] = solved_two

    for step in peers:
        sel_copy(step).wait_send()
    for piece in range(5):
        for step in range(size_z):
            gather_copy(piece, step).wait_send()
        for step in range(1, size_z):
            forward_copy(piece, step).wait_send()
    for which in range(2):
        pair_copy(which).wait_send()
        half_copy(which).wait_send()
        for step in range(1, groups):
            group_copy(which, step).wait_send()
    for item in range(5):
        @pl.when(my_row == owners[item])
        def _(item=item):
            for step in range(groups):
                item_copy(item, step, item_source(item)).wait_send()

        @pl.when((group > 0) & (core == owners[item]))
        def _(item=item):
            item_copy(item, 0, item_place(item)).wait_send()


def on_device(matrix, panel_one, panel_two, pivots_one, pivots_two):
    process_rows = lax.axis_size("prow")
    process_cols = lax.axis_size("pcol")
    shard, rows_dev = panel_one.shape
    width = pivots_one.shape[0]
    cols = matrix.shape[1]
    vmem = pl.BlockSpec(memory_space=pltpu.VMEM)
    hbm = pl.BlockSpec(memory_space=pltpu.HBM)
    dma = pltpu.SemaphoreType.DMA
    assert rows_dev > width and shard * process_cols == width
    assert process_cols % 2 == 0 and process_rows % 2 == 0
    size_z = process_cols // 2
    groups = process_rows // 2
    half = width // 2
    return pl.pallas_call(
        functools.partial(body, process_rows, process_cols),
        out_shape=jax.ShapeDtypeStruct(matrix.shape, BF16),
        in_specs=[hbm] * 3 + [vmem] * 2,
        out_specs=vmem,
        scratch_shapes=[
            pltpu.VMEM((rows_dev, cols), BF16),
            pltpu.VMEM((3, process_cols, shard, width), BF16),
            pltpu.VMEM((2, process_cols, shard, rows_dev - width), BF16),
            pltpu.VMEM((shard, width), BF16),
            pltpu.VMEM((process_rows, shard, width), BF16),
            [pltpu.VMEM((3, process_cols, shard, width), BF16), pltpu.VMEM((2, width, cols), BF16)],
            pltpu.VMEM((2, 2, half, cols), BF16),
            pltpu.VMEM((2, half, cols), BF16),
            pltpu.VMEM((2, groups, half, cols), BF16),
            pltpu.VMEM((2, 2, half, cols), BF16),
            dma((5,)),
            dma((3, size_z)), dma((3, process_cols)), dma((3, size_z)),
            dma((2, size_z)), dma((2, process_cols)), dma((2, size_z)),
            dma((process_rows,)), dma((process_rows,)),
            dma((5, groups)), dma((5,)),
            dma((2,)), dma((2,)),
            dma((2, groups)), dma((2, groups)),
            dma((2,)), dma((2,)),
        ],
        compiler_params=pltpu.CompilerParams(
            collective_id=0, has_side_effects=True, vmem_limit_bytes=63 * 1024 * 1024
        ),
    )(matrix, panel_one, panel_two, pivots_one.reshape(1, width), pivots_two.reshape(1, width))


def solution(mesh):
    placed = (P("prow", "pcol"), P("pcol", "prow"), P("pcol", "prow"), P(), P())
    return jax.shard_map(
        on_device, mesh=mesh, in_specs=placed, out_specs=P("prow", "pcol"), check_vma=False
    )
```

```python
import functools

import jax
import jax.numpy as jnp
from jax import lax
from jax.experimental import pallas as pl
from jax.experimental.pallas import tpu as pltpu
from jax.sharding import PartitionSpec as P

F32 = jnp.float32
BF16 = jnp.bfloat16
ROW_ROW = (((0,), (0,)), ((), ()))


def dot(a, b):
    return jnp.dot(a, b, preferred_element_type=F32)


def dot_t(a, b):
    return lax.dot_general(a, b, ROW_ROW, preferred_element_type=F32)


def halves(a):
    high = a.astype(BF16)
    return high, (a - high.astype(F32)).astype(BF16)


def dot_split(a, b):
    a_high, a_low = halves(a)
    b_high, b_low = halves(b)
    return dot(a_high, b_high) + (dot(a_high, b_low) + dot(a_low, b_high))


def unit_inverses(diagonals):
    extent = diagonals[0].shape[0]
    row = lax.broadcasted_iota(jnp.int32, (extent, extent), 0)
    col = lax.broadcasted_iota(jnp.int32, (extent, extent), 1)
    stricts = [jnp.where(row > col, d.astype(F32).T, 0.0) for d in diagonals]
    powers = [dot(s.astype(BF16), s.astype(BF16)) for s in stricts]
    results = [jnp.where(row == col, 1.0, 0.0) - s for s in stricts]
    repeats = (extent - 1).bit_length() - 1
    for repeat in range(repeats):
        if repeat == repeats - 1:
            return [r + dot_split(r, p) for r, p in zip(results, powers)]
        both = [dot_split(jnp.concatenate([r, p], axis=0), p) for r, p in zip(results, powers)]
        results = [r + b[:extent] for r, b in zip(results, both)]
        powers = [b[extent:] for b in both]


def unit_inverse(diagonal):
    extent = diagonal.shape[0]
    row = lax.broadcasted_iota(jnp.int32, (extent, extent), 0)
    col = lax.broadcasted_iota(jnp.int32, (extent, extent), 1)
    strict = jnp.where(row > col, diagonal.astype(F32).T, 0.0)
    exact = strict.astype(BF16)
    powered = dot(exact, exact)
    result = jnp.where(row == col, 1.0, 0.0) - strict
    repeats = (extent - 1).bit_length() - 1
    for repeat in range(repeats):
        if repeat == repeats - 1:
            return result + dot_split(result, powered)
        both = dot_split(jnp.concatenate([result, powered], axis=0), powered)
        result, powered = result + both[:extent], both[extent:]
    return result


def solve(inverse, incoming):
    high, low = halves(inverse)
    return (dot(high, incoming) + dot(low, incoming)).astype(BF16)


def onehot(a, b):
    return (a == b).astype(F32)


def body(
    process_rows, process_cols,
    matrix_hbm, one_hbm, two_hbm, piv_one_hbm, piv_two_hbm, out,
    piv_one, piv_two, matrix, head, tail, sent_sel, sel_in, item_in,
    sent_rows, pair_rows, group_rows, full_rows,
    l_sem, gh_send, gh_recv, fh_send, gt_send, gt_recv, ft_send, s_send, s_recv, i_send, i_recv,
    p_send, p_recv, q_send, q_recv, h_send, h_recv,
):
    width = piv_one.shape[1]
    rows_dev = matrix.shape[0]
    shard = one_hbm.shape[0]
    half = width // 2
    size_z = process_cols // 2
    groups = process_rows // 2
    my_row = lax.axis_index("prow")
    my_col = lax.axis_index("pcol")
    my_z, my_x = my_col // 2, my_col % 2
    x_peer = my_z * 2 + (1 - my_x)
    group, core = my_row // 2, my_row % 2
    pair = group * 2 + (1 - core)
    mesh_ids = pl.DeviceIdType.MESH

    def row_peer(step):
        return lax.rem(my_row + step, process_rows)

    def group_peer(step):
        return lax.rem(group + step, groups) * 2 + core

    def z_peer(step):
        return lax.rem(my_z + step, size_z) * 2 + my_x

    barrier = pltpu.get_barrier_semaphore()
    for step in range(1, process_rows):
        pl.semaphore_signal(barrier, 1, device_id={"prow": row_peer(step)}, device_id_type=mesh_ids)
    for step in range(1, size_z):
        pl.semaphore_signal(barrier, 1, device_id={"pcol": z_peer(step)}, device_id_type=mesh_ids)
    pl.semaphore_signal(barrier, 1, device_id={"pcol": x_peer}, device_id_type=mesh_ids)

    first, rest = pl.ds(0, width), pl.ds(width, rows_dev - width)
    loads = [
        pltpu.make_async_copy(one_hbm.at[:, first], head.at[0, my_col], l_sem.at[0]),
        pltpu.make_async_copy(one_hbm.at[:, rest], tail.at[0, my_col], l_sem.at[1]),
        pltpu.make_async_copy(two_hbm.at[:, first], head.at[1, my_col], l_sem.at[2]),
        pltpu.make_async_copy(matrix_hbm, matrix, l_sem.at[3]),
        pltpu.make_async_copy(two_hbm.at[:, rest], tail.at[1, my_col], l_sem.at[4]),
    ]
    names = [
        pltpu.make_async_copy(piv_one_hbm, piv_one, l_sem.at[5]),
        pltpu.make_async_copy(piv_two_hbm, piv_two, l_sem.at[6]),
    ]
    for load in names:
        load.start()
    for load in loads:
        load.start()

    for load in names:
        load.wait()

    local = lax.broadcasted_iota(jnp.int32, (rows_dev, width), 0)
    logical = (local // width * process_rows + my_row) * width + local % width
    hit_one = onehot(logical, piv_one[...])
    hit_two = onehot(logical, piv_two[...])
    pick_one, pick_two = hit_one.astype(BF16), hit_two.astype(BF16)
    for load in loads:
        load.wait()
    sent_sel[...] = (dot(head[0, my_col], pick_two[:width]) + dot(tail[0, my_col], pick_two[width:])).astype(BF16)
    for which, pick in enumerate((pick_one, pick_two)):
        sent_rows[which] = dot_t(pick, matrix[...]).astype(BF16).reshape(2, half, matrix.shape[1])

    pl.semaphore_wait(barrier, process_rows - 1 + size_z)

    def remote(src, dst, send, recv, device):
        return pltpu.make_async_remote_copy(
            src_ref=src, dst_ref=dst, send_sem=send, recv_sem=recv,
            device_id=device, device_id_type=mesh_ids,
        )

    def slot_of(piece, col):
        if piece < 3:
            return head.at[piece, col], gh_send.at[piece], gh_recv.at[piece, col], fh_send.at[piece]
        return tail.at[piece - 3, col], gt_send.at[piece - 3], gt_recv.at[piece - 3, col], ft_send.at[piece - 3]

    def gather_copy(piece, step):
        slot, send, recv, _ = slot_of(piece, my_col)
        return remote(slot, slot, send.at[step], recv, {"pcol": z_peer(step) if step else x_peer})

    def forward_copy(piece, step):
        slot, _, recv, send = slot_of(piece, z_peer(step))
        return remote(slot, slot, send.at[step], recv, {"pcol": x_peer})

    def gather(piece):
        for step in reversed(range(size_z)):
            gather_copy(piece, step).start()

    def arrive(piece, col):
        slot, send, recv, _ = slot_of(piece, col)
        remote(slot, slot, send.at[0], recv, {"pcol": x_peer}).wait_recv()

    def take_z(piece):
        for step in range(1, size_z):
            arrive(piece, z_peer(step))
            forward_copy(piece, step).start()

    def take_x(piece):
        for step in range(size_z):
            arrive(piece, lax.rem(my_z + step, size_z) * 2 + (1 - my_x))

    def flat(block):
        return block.reshape(process_cols * shard, block.shape[-1])

    def sel_copy(step):
        return remote(sent_sel, sel_in.at[my_row], s_send.at[step], s_recv.at[my_row], {"prow": row_peer(step)})

    owners = (0, 1, 1, 0, 1)

    def item_source(item):
        if item < 3:
            return head.at[(0, 1, 0)[item]]
        return matrix.at[first, :]

    def item_place(item):
        return item_in[0].at[item] if item < 3 else item_in[1].at[item - 3]

    def item_copy(item, step, source):
        device = {"prow": group_peer(step) if step else pair}
        return remote(source, item_place(item), i_send.at[item, step], i_recv.at[item], device)

    def send_item(item):
        @pl.when(my_row == owners[item])
        def _():
            for step in range(groups):
                item_copy(item, step, item_source(item)).start()
            if item < 3:
                item_in[0][item] = head[(0, 1, 0)[item]]
            else:
                item_in[1][item - 3] = matrix[first, :]

    def take_item(item):
        @pl.when(my_row != owners[item])
        def _():
            item_copy(item, 0, item_place(item)).wait_recv()

        @pl.when((group > 0) & (core == owners[item]))
        def _():
            item_copy(item, 0, item_place(item)).start()

    def pair_copy(which):
        return remote(sent_rows.at[which, 1 - core], pair_rows.at[which], p_send.at[which], p_recv.at[which], {"prow": pair})

    def group_copy(which, step):
        return remote(
            sent_rows.at[which, core], group_rows.at[which, group],
            q_send.at[which, step], q_recv.at[which, group], {"prow": group_peer(step)},
        )

    def half_copy(which):
        return remote(
            full_rows.at[which, core], full_rows.at[which, core], h_send.at[which], h_recv.at[which], {"prow": pair}
        )

    def sum_pair(which):
        slot = pair_rows.at[which]
        remote(slot, slot, p_send.at[which], p_recv.at[which], {"prow": pair}).wait_recv()
        total = sent_rows[which, core].astype(F32) + pair_rows[which].astype(F32)
        sent_rows[which, core] = total.astype(BF16)
        for step in range(1, groups):
            group_copy(which, step).start()

    def sum_groups(which):
        total = sent_rows[which, core].astype(F32)
        for step in range(1, groups):
            source = lax.rem(group + step, groups)
            slot = group_rows.at[which, source]
            remote(slot, slot, q_send.at[which, 0], q_recv.at[which, source], {"prow": pair}).wait_recv()
            total = total + group_rows[which, source].astype(F32)
        full_rows[which, core] = total.astype(BF16)
        half_copy(which).start()

    def chosen(which):
        slot = full_rows.at[which, 1 - core]
        remote(slot, slot, h_send.at[which], h_recv.at[which], {"prow": pair}).wait_recv()
        return full_rows[which].reshape(width, full_rows.shape[-1])

    peers = range(1, process_rows)
    gather(0)
    gather(1)
    for step in peers:
        sel_copy(step).start()
    for which in range(2):
        pair_copy(which).start()
    gather(3)
    take_z(0)
    take_z(1)
    sum_pair(0)
    sum_pair(1)
    selected = sent_sel[...].astype(F32)
    for step in peers:
        source = row_peer(step)
        slot = sel_in.at[source]
        remote(slot, slot, s_send.at[0], s_recv.at[source], {"prow": source}).wait_recv()
        selected = selected + sel_in[source].astype(F32)
    head[2, my_col] = selected.astype(BF16)
    gather(2)
    gather(4)
    take_x(0)
    send_item(0)
    take_x(1)
    send_item(1)
    sum_groups(0)
    sum_groups(1)
    send_item(3)
    send_item(2)
    send_item(4)
    take_z(3)
    take_z(2)
    take_item(0)
    take_item(1)
    take_z(4)
    inverse_one, inverse_two = unit_inverses([flat(item_in[0][0]), flat(item_in[0][1])])
    take_item(3)
    take_item(2)
    take_item(4)

    solved_one = solve(inverse_one, chosen(0))
    leaving_one = item_in[1][0]

    first_across = jnp.broadcast_to(piv_one[...], (width, width))
    second_down = jnp.broadcast_to(piv_two[...].astype(F32), (width, width)).T.astype(jnp.int32)
    block_down = width + lax.broadcasted_iota(jnp.int32, (width, width), 0)

    def after_one(base, names, columns):
        match = onehot(names, first_across)
        moved = jnp.sum(match, axis=1, keepdims=True)
        swapped = base.astype(F32) * (1.0 - moved) + dot(match.astype(BF16), leaving_one)
        return (swapped - dot_t(columns, solved_one)).astype(BF16)

    take_x(2)
    incoming_two = after_one(chosen(1), second_down, flat(head[2]))
    leaving_two = after_one(item_in[1][1], block_down, flat(item_in[0][2]))
    solved_two = solve(inverse_two, incoming_two)

    moved_one = jnp.sum(hit_one, axis=1, keepdims=True)
    moved_two = jnp.sum(hit_two, axis=1, keepdims=True)
    swapped = matrix[...].astype(F32) * (1.0 - moved_one) + dot(pick_one, leaving_one)

    def times(which, solved):
        return jnp.concatenate([dot_t(flat(head[which]), solved), dot_t(flat(tail[which]), solved)], axis=0)

    take_x(3)
    current = (swapped - times(0, solved_one)).astype(BF16).astype(F32)
    swapped = current * (1.0 - moved_two) + dot(pick_two, leaving_two)
    take_x(4)
    out[...] = (swapped - times(1, solved_two)).astype(BF16)

    @pl.when(my_row == 0)
    def _():
        out[first, :] = solved_one

    @pl.when(my_row == 1)
    def _():
        out[first, :] = solved_two

    for step in peers:
        sel_copy(step).wait_send()
    for piece in range(5):
        for step in range(size_z):
            gather_copy(piece, step).wait_send()
        for step in range(1, size_z):
            forward_copy(piece, step).wait_send()
    for which in range(2):
        pair_copy(which).wait_send()
        half_copy(which).wait_send()
        for step in range(1, groups):
            group_copy(which, step).wait_send()
    for item in range(5):
        @pl.when(my_row == owners[item])
        def _(item=item):
            for step in range(groups):
                item_copy(item, step, item_source(item)).wait_send()

        @pl.when((group > 0) & (core == owners[item]))
        def _(item=item):
            item_copy(item, 0, item_place(item)).wait_send()


def on_device(matrix, panel_one, panel_two, pivots_one, pivots_two):
    process_rows = lax.axis_size("prow")
    process_cols = lax.axis_size("pcol")
    shard, rows_dev = panel_one.shape
    width = pivots_one.shape[0]
    cols = matrix.shape[1]
    vmem = pl.BlockSpec(memory_space=pltpu.VMEM)
    hbm = pl.BlockSpec(memory_space=pltpu.HBM)
    dma = pltpu.SemaphoreType.DMA
    assert rows_dev > width and shard * process_cols == width
    assert process_cols % 2 == 0 and process_rows % 2 == 0
    size_z = process_cols // 2
    groups = process_rows // 2
    half = width // 2
    return pl.pallas_call(
        functools.partial(body, process_rows, process_cols),
        out_shape=jax.ShapeDtypeStruct(matrix.shape, BF16),
        in_specs=[hbm] * 5,
        out_specs=vmem,
        scratch_shapes=[
            pltpu.VMEM((1, width), jnp.int32),
            pltpu.VMEM((1, width), jnp.int32),
            pltpu.VMEM((rows_dev, cols), BF16),
            pltpu.VMEM((3, process_cols, shard, width), BF16),
            pltpu.VMEM((2, process_cols, shard, rows_dev - width), BF16),
            pltpu.VMEM((shard, width), BF16),
            pltpu.VMEM((process_rows, shard, width), BF16),
            [pltpu.VMEM((3, process_cols, shard, width), BF16), pltpu.VMEM((2, width, cols), BF16)],
            pltpu.VMEM((2, 2, half, cols), BF16),
            pltpu.VMEM((2, half, cols), BF16),
            pltpu.VMEM((2, groups, half, cols), BF16),
            pltpu.VMEM((2, 2, half, cols), BF16),
            dma((7,)),
            dma((3, size_z)), dma((3, process_cols)), dma((3, size_z)),
            dma((2, size_z)), dma((2, process_cols)), dma((2, size_z)),
            dma((process_rows,)), dma((process_rows,)),
            dma((5, groups)), dma((5,)),
            dma((2,)), dma((2,)),
            dma((2, groups)), dma((2, groups)),
            dma((2,)), dma((2,)),
        ],
        compiler_params=pltpu.CompilerParams(
            collective_id=0, has_side_effects=True, vmem_limit_bytes=63 * 1024 * 1024
        ),
    )(matrix, panel_one, panel_two, pivots_one.reshape(1, width), pivots_two.reshape(1, width))


def solution(mesh):
    placed = (P("prow", "pcol"), P("pcol", "prow"), P("pcol", "prow"), P(), P())
    return jax.shard_map(
        on_device, mesh=mesh, in_specs=placed, out_specs=P("prow", "pcol"), check_vma=False
    )
```
